32 devices in a mesh: member: 2 (over x), fsdp: 16 (over z, y, core).
Axes of the slice: x: 2, y: 2, z: 4, core: 2. Of those that a mesh axis runs over, the one named last changes fastest.
Arguments:
- context: bfloat16 [4, 2048, 2048], P(None, 'fsdp', 'member'), may hold values from -6 to 6
- residual: bfloat16 [2048, 2048], P('fsdp', 'member'), may hold values from -6 to 6
- out_weight: bfloat16 [2048, 2048], P('fsdp', 'member'), may hold values from -0.1875 to 0.1875
- in_factor: bfloat16 [4, 2048], P(None, 'member'), may hold values from 0.25 to 1.75
- out_factor: bfloat16 [4, 2048], P(None, 'member'), may hold values from 0.25 to 1.75
- cotangent: bfloat16 [4, 2048, 2048], P(None, 'fsdp', 'member'), may hold values from -0.796875 to 0.796875
Outputs:
- hidden: bfloat16 [4, 2048, 2048], P(None, 'fsdp', 'member')
- grad_context: bfloat16 [4, 2048, 2048], P(None, 'fsdp', 'member')
- grad_weight: float32 [2048, 2048], P('fsdp', 'member')
- grad_in_factor: float32 [4, 2048], P(None, 'member')
- grad_out_factor: float32 [4, 2048], P(None, 'member')
- grad_residual: float32 [2048, 2048], P('fsdp', 'member')
The draws below stay inside these ranges and needn't reach their ends.
All inputs are finite; a program needn't handle non-finite values.
Results may differ from the reference program's by a relative error of at most 0.013.
Values may be sent and summed in bfloat16 or wider, within the bound.
A program may use at most 64 MiB of HBM per device.

```python
import jax
import jax.numpy as jnp
from jax import lax

INNER = 2048
DW = 2048
ENSEMBLE = 4
TOKENS = 2048
N_MEMBER = 2


def raised(array, own_key, source, target, blocks, factor):
    owner, partner = [(jnp.arange(array.shape[dim]) // (array.shape[dim] // blocks)).reshape([-1 if axis == dim else 1 for axis in range(array.ndim)]) for dim in (source, target)]
    chosen = jax.random.permutation(own_key, blocks)[partner]
    strong = (owner == chosen) | (owner == (partner + blocks // 2) % blocks)
    return jnp.where(strong, factor * array, array)


def shard_levels(rng, shape, pieces, least, high):
    factor_of, own = 1.0, jax.random.fold_in(rng, 6)
    for dim, parts in pieces:
        heights = jnp.exp(jax.random.uniform(jax.random.fold_in(own, dim), (parts,), jnp.float32, least / len(pieces), high / len(pieces)))
        factor_of = factor_of * jnp.repeat(heights, shape[dim] // parts).reshape([-1 if axis == dim else 1 for axis in range(len(shape))])
    return factor_of


def gaussian(rng, extent, scale, most, split=(), held_as=jnp.bfloat16):
    result = jax.random.normal(rng, extent, jnp.float32) * scale
    if len(split) > 0:
        result = shard_levels(rng, extent, split, -0.22, 0.18) * result
    return jnp.clip(result, min=-most, max=most).astype(held_as)


def gaussian_with(stream_key, dims, deviation, limit, shards, heavy, dtype=jnp.bfloat16):
    result = deviation * jax.random.normal(stream_key, dims, jnp.float32)
    if shards:
        result = result * shard_levels(stream_key, dims, shards, -0.22, 0.18)
    return jnp.clip(raised(result, jax.random.fold_in(stream_key, 3), *heavy), -limit, limit).astype(dtype)


def setup_inputs(seed: int = 0) -> dict:
    keys = jax.random.split(jax.random.key(seed), 7)
    return {
        "context": gaussian_with(keys[0], (ENSEMBLE, TOKENS, INNER), 1.0, 6.0, ((1, 16), (2, 2)), (1, 2, 16, 2.0)),
        "residual": gaussian(keys[1], (TOKENS, DW), 1.0, 6.0, ((0, 16), (1, 2))),
        "out_weight": gaussian_with(keys[2], (INNER, DW), INNER ** -0.5, 0.1875, ((0, 16), (1, 2)), (1, 0, 16, 2.0)),
        "in_factor": jnp.clip(1.0 + 0.15 * jax.random.normal(keys[3], (ENSEMBLE, INNER), jnp.float32), 0.25, 1.75).astype(jnp.bfloat16),
        "out_factor": jnp.clip(1.0 + 0.15 * jax.random.normal(keys[4], (ENSEMBLE, DW), jnp.float32), 0.25, 1.75).astype(jnp.bfloat16),
        "cotangent": gaussian(keys[5], (ENSEMBLE, TOKENS, DW), 0.1, 0.796875, ((1, 16), (2, 2))),
    }


def reference(context, residual, out_weight, in_factor, out_factor, cotangent):
    resid_wide = residual.astype(jnp.float32)
    block_width = DW // N_MEMBER

    def member_step(running, member_items):
        weight_sum, resid_sum = running
        context_rows, in_scale, out_scale, grad_rows = member_items
        in_wide = in_scale.astype(jnp.float32)
        out_wide = out_scale.astype(jnp.float32)
        scaled_context = (context_rows.astype(jnp.float32) * in_wide).astype(jnp.bfloat16)
        scaled_grad = (grad_rows.astype(jnp.float32) * out_wide).astype(jnp.bfloat16)
        projected = jnp.dot(scaled_context, out_weight, preferred_element_type=jnp.float32)
        hidden = (resid_wide + projected * out_wide).astype(jnp.bfloat16)
        backward = jnp.zeros((TOKENS, INNER), jnp.float32)
        for block_index in range(N_MEMBER):
            lower = block_index * block_width
            upper = lower + block_width
            partial_value = jnp.dot(scaled_grad[:, lower:upper], out_weight[:, lower:upper].T, preferred_element_type=jnp.float32).astype(jnp.bfloat16)
            backward = backward + partial_value.astype(jnp.float32)
        grad_context = (backward * in_wide).astype(jnp.bfloat16)
        grad_in = jnp.sum(context_rows.astype(jnp.float32) * backward, axis=0)
        grad_out = jnp.sum(grad_rows.astype(jnp.float32) * projected, axis=0)
        weight_sum = weight_sum + jnp.dot(scaled_context.T, scaled_grad, preferred_element_type=jnp.float32)
        resid_sum = resid_sum + grad_rows.astype(jnp.float32)
        return (weight_sum, resid_sum), (hidden, grad_context, grad_in, grad_out)

    start_state = (jnp.zeros((INNER, DW), jnp.float32), jnp.zeros((TOKENS, DW), jnp.float32))
    final_state, outputs = lax.scan(member_step, start_state, (context, in_factor, out_factor, cotangent))
    grad_weight, grad_residual = final_state
    hidden, grad_context, grad_in_factor, grad_out_factor = outputs
    return hidden, grad_context, grad_weight, grad_in_factor, grad_out_factor, grad_residual
```

```python
import functools

import jax
import jax.numpy as jnp
from jax import lax
from jax.experimental import pallas as pl
from jax.experimental.pallas import tpu as pltpu
from jax.sharding import PartitionSpec as P

F32 = jnp.float32
BF16 = jnp.bfloat16


def general(context, residual, out_weight, in_factor, out_factor, cotangent):
    in_wide = in_factor.astype(jnp.float32)
    out_wide = out_factor.astype(jnp.float32)
    scaled_local = (context.astype(jnp.float32) * in_wide[:, None, :]).astype(jnp.bfloat16)
    scaled_grad = (cotangent.astype(jnp.float32) * out_wide[:, None, :]).astype(jnp.bfloat16)
    scaled_context = lax.all_gather(scaled_local, "member", axis=2, tiled=True)
    weight = lax.all_gather(out_weight, "fsdp", axis=0, tiled=True)
    projected = jnp.einsum(
        "eti,id->etd", scaled_context, weight, preferred_element_type=jnp.float32
    )
    partial_value = jnp.einsum(
        "etd,id->eti", scaled_grad, weight, preferred_element_type=jnp.float32
    )
    hidden = (residual.astype(jnp.float32)[None] + projected * out_wide[:, None, :]).astype(
        jnp.bfloat16
    )
    backward = lax.psum_scatter(
        partial_value.astype(jnp.bfloat16), "member", scatter_dimension=2, tiled=True
    ).astype(jnp.float32)
    grad_context = (backward * in_wide[:, None, :]).astype(jnp.bfloat16)
    grad_in_local = jnp.sum(context.astype(jnp.float32) * backward, axis=1)
    grad_out_local = jnp.sum(cotangent.astype(jnp.float32) * projected, axis=1)
    grad_in, grad_out = lax.psum((grad_in_local, grad_out_local), "fsdp")
    grad_block = jnp.einsum(
        "eti,etd->id", scaled_context, scaled_grad, preferred_element_type=jnp.float32
    )
    grad_weight = lax.psum_scatter(grad_block, "fsdp", scatter_dimension=0, tiled=True)
    grad_residual = jnp.sum(cotangent.astype(jnp.float32), axis=0)
    return (hidden, grad_context, grad_weight, grad_in, grad_out, grad_residual)


def kernel(
    C,
    ctx, res, w, inf, outf, cot,
    hid, gc, gw, gi, go, gr,
    sc, sg, wb, proj, part, xrecv, gall, psend, precv, rsend, rrecv, arb, arr,
    cx_sem, ag_ss, ag_rs, pt_ss, pt_rs, px_ss, px_rs, ps_ss, ps_rs, rs_ss, rs_rs, ar_ss, ar_rs,
):
    E, T, H = ctx.shape
    M = E * T
    R = w.shape[0]
    R2 = 2 * R
    half = C // 2
    far = C // 2
    bits = []
    b = 1
    while b < 2 * C:
        bits.append(b)
        b *= 2

    m = lax.axis_index("member")
    f = lax.axis_index("fsdp")
    c = f % 2
    q = f // 2
    p = (1 - q % 2) * (q // 2) + (q % 2) * (C - 1 - q // 2)

    def chip_at(offset):
        pos = (p + offset + C) % C
        y = pos // half
        return 2 * ((1 - y) * pos + y * (C - 1 - pos)) + y

    peer = (1 - m, f)
    partner = (m, q * 2 + 1 - c)
    nxt = (m, chip_at(1) * 2 + c)
    prv = (m, chip_at(-1) * 2 + c)
    side = (nxt, prv)
    sign = (1, -1)
    flips = [(m, f + bit * (1 - 2 * ((f // bit) % 2))) for bit in bits]

    def rc(src, dst, ss, rs, dev):
        return pltpu.make_async_remote_copy(
            src_ref=src, dst_ref=dst, send_sem=ss, recv_sem=rs,
            device_id=dev, device_id_type=pl.DeviceIdType.MESH,
        )

    barrier = pltpu.get_barrier_semaphore()
    greet = [peer, nxt, prv] + flips
    for dev in greet:
        pl.semaphore_signal(barrier, inc=1, device_id=dev, device_id_type=pl.DeviceIdType.MESH)

    inw = inf[...].astype(F32)
    outw = outf[...].astype(F32)
    for e in range(E):
        v = (ctx[e].astype(F32) * inw[e:e + 1]).astype(BF16)
        for j in range(half):
            sc[m * half + j, e * T:(e + 1) * T, :] = v[:, j * R2:(j + 1) * R2]

    pl.semaphore_wait(barrier, len(greet))

    def rows_of(core):
        return pl.ds(pl.multiple_of(core * R, R), R)

    cx = rc(sc.at[pl.ds(m * half, half)], sc.at[pl.ds(m * half, half)], cx_sem.at[0], cx_sem.at[1], peer)

    def ag_rows(d, s):
        if s < far:
            return rows_of(c)
        return pl.ds(pl.multiple_of(c * R + d * (R // 2), R // 2), R // 2)

    def ag(d, s, shift):
        qq = chip_at(-sign[d] * (s - 1 + shift))
        dst = wb.at[qq, ag_rows(d, s)]
        src = w if (s == 1 and shift == 0) else dst
        return rc(src, dst, ag_ss.at[d, s - 1], ag_rs.at[d, s - 1], side[d])

    def pt(k, offset, mine):
        qq = chip_at(offset)
        dst = wb.at[qq, rows_of(c if mine else 1 - c)]
        src = w if (mine and k == 0) else dst
        return rc(src, dst, pt_ss.at[k], pt_rs.at[k], partner)

    sends = []

    def go_send(copy):
        copy.start()
        sends.append(copy)

    go_send(ag(0, 1, 0))
    go_send(ag(1, 1, 0))
    go_send(cx)
    go_send(pt(0, 0, True))
    wb[q, rows_of(c), :] = w[...]

    for e in range(E):
        sg[e * T:(e + 1) * T, :] = (cot[e].astype(F32) * outw[e:e + 1]).astype(BF16)
    proj[...] = jnp.zeros(proj.shape, F32)

    def px(qq):
        return rc(part.at[qq], xrecv.at[qq % half], px_ss.at[qq % half], px_rs.at[qq % half], peer)

    def ps(qq):
        return rc(psend.at[qq], precv.at[qq], ps_ss.at[qq], ps_rs.at[qq], partner)

    def gw_half(h):
        def body(j, carry):
            qq = h * half + j
            g = lax.dot_general(sc[qq], sg[...], (((0,), (0,)), ((), ())), preferred_element_type=F32)
            gall[qq, 0] = g[:R]
            gall[qq, 1] = g[R:]
            psend[qq] = gall[qq, 1 - c].astype(BF16)
            ps(qq).start()
            return carry
        lax.fori_loop(0, half, body, 0)

    def project(qq):
        proj[...] += jnp.dot(sc[qq], wb[qq], preferred_element_type=F32)

    def process(offsets):
        def body(j, carry):
            off = offsets[0] if len(offsets) == 1 else offsets[0] + j * (offsets[1] - offsets[0])
            qq = chip_at(off)
            part[qq] = lax.dot_general(
                sg[...], wb[qq], (((1,), (1,)), ((), ())), preferred_element_type=F32
            ).astype(BF16)

            @pl.when(qq // half != m)
            def _():
                px(qq).start()

            @pl.when(qq // half == m)
            def _():
                project(qq)
            return carry
        lax.fori_loop(0, len(offsets), body, 0)

    gw_half(m)
    pt(0, 0, False).wait_recv()
    process([0])
    for s in range(1, far):
        for d in range(2):
            ag(d, s, 1).wait_recv()
            go_send(ag(d, s + 1, 0))
            go_send(pt(d * (far - 1) + s, -sign[d] * s, True))
        if s == 1:
            gr[...] = jnp.sum(cot[...].astype(F32), axis=0)
        for d in range(2):
            pt(d * (far - 1) + s, -sign[d] * s, False).wait_recv()
        process([-s, s])
    ag(0, far, 1).wait_recv()
    ag(1, far, 1).wait_recv()
    go_send(pt(2 * far - 1, far, True))
    pt(2 * far - 1, far, False).wait_recv()
    process([far])

    rc(sc.at[pl.ds((1 - m) * half, half)], sc.at[pl.ds((1 - m) * half, half)],
       cx_sem.at[0], cx_sem.at[1], peer).wait_recv()
    gw_half(1 - m)

    def rs(d, k):
        rows = pl.ds(d * (R // 2), R // 2) if k == 0 else pl.ds(0, R)
        return rc(rsend.at[d, k, rows], rrecv.at[d, k, rows], rs_ss.at[d, k], rs_rs.at[d, k], side[d])

    def chip_sum(qq):
        return gall[qq, c] + precv[qq].astype(F32)

    qf = chip_at(far)
    ps(qf).wait_recv()
    v = chip_sum(qf).astype(BF16)
    for d in range(2):
        lo = d * (R // 2)
        rsend[d, 0, lo:lo + R // 2, :] = v[lo:lo + R // 2]
        go_send(rs(d, 0))

    def rs_step(k):
        for d in range(2):
            qq = chip_at(sign[d] * (far - k))
            ps(qq).wait_recv()
            v = chip_sum(qq)
            rs(d, k - 1).wait_recv()
            if k == 1:
                lo = d * (R // 2)
                other = (1 - d) * (R // 2)
                rsend[d, k, lo:lo + R // 2, :] = (
                    v[lo:lo + R // 2] + rrecv[d, 0, lo:lo + R // 2, :].astype(F32)
                ).astype(BF16)
                rsend[d, k, other:other + R // 2, :] = v[other:other + R // 2].astype(BF16)
            else:
                rsend[d, k] = (v + rrecv[d, k - 1].astype(F32)).astype(BF16)
            go_send(rs(d, k))

    def project_rest(lo, hi):
        def body(j, carry):
            project((1 - m) * half + j)
            return carry
        lax.fori_loop(lo, hi, body, 0)

    mid = half // 2
    project_rest(0, mid)
    rs_step(1)
    project_rest(mid, half)
    rs_step(2)
    resw = res[...].astype(F32)
    for e in range(E):
        pe = proj[e * T:(e + 1) * T, :]
        hid[e] = (resw + pe * outw[e:e + 1]).astype(BF16)
        arb[0, E + e:E + e + 1, :] = jnp.sum(cot[e].astype(F32) * pe, axis=0, keepdims=True)
    for k in range(3, far):
        rs_step(k)

    for j in range(half):
        qq = m * half + j
        rc(xrecv.at[j], xrecv.at[j], px_ss.at[j], px_rs.at[j], peer).wait_recv()
        cols = slice(j * R2, (j + 1) * R2)
        for e in range(E):
            rows = slice(e * T, (e + 1) * T)
            be = part[qq, rows, :].astype(F32) + xrecv[j, rows, :].astype(F32)
            gc[e, :, cols] = (be * inw[e:e + 1, cols]).astype(BF16)
            arb[0, e:e + 1, cols] = jnp.sum(ctx[e, :, cols].astype(F32) * be, axis=0, keepdims=True)

    def ar(i):
        return rc(arb.at[i], arr.at[i], ar_ss.at[i], ar_rs.at[i], flips[i])

    go_send(ar(0))
    ps(q).wait_recv()
    own = chip_sum(q)
    rs(0, far - 1).wait_recv()
    rs(1, far - 1).wait_recv()
    gw[...] = own + rrecv[0, far - 1].astype(F32) + rrecv[1, far - 1].astype(F32)
    for i in range(len(bits)):
        ar(i).wait_recv()
        total = arb[i] + arr[i]
        if i + 1 < len(bits):
            arb[i + 1] = total
            go_send(ar(i + 1))
        else:
            gi[...] = total[:E]
            go[...] = total[E:]

    for copy in sends:
        copy.wait_send()

    def drain(j, carry):
        ps(j).wait_send()
        return carry
    lax.fori_loop(0, C, drain, 0)
    for j in range(half):
        rc(part.at[(1 - m) * half + j], xrecv.at[j], px_ss.at[j], px_rs.at[j], peer).wait_send()


def fused(C, context, residual, out_weight, in_factor, out_factor, cotangent):
    E, T, H = context.shape
    M = E * T
    R = out_weight.shape[0]
    half = C // 2
    far = half
    steps = (2 * C).bit_length() - 1
    vm = pl.BlockSpec(memory_space=pltpu.VMEM)
    dma = pltpu.SemaphoreType.DMA
    shape = jax.ShapeDtypeStruct
    return pl.pallas_call(
        functools.partial(kernel, C),
        out_shape=(
            shape((E, T, H), BF16),
            shape((E, T, H), BF16),
            shape((R, H), F32),
            shape((E, H), F32),
            shape((E, H), F32),
            shape((T, H), F32),
        ),
        in_specs=[vm] * 6,
        out_specs=tuple([vm] * 6),
        scratch_shapes=[
            pltpu.VMEM((C, M, 2 * R), BF16),
            pltpu.VMEM((M, H), BF16),
            pltpu.VMEM((C, 2 * R, H), BF16),
            pltpu.VMEM((M, H), F32),
            pltpu.VMEM((C, M, 2 * R), BF16),
            pltpu.VMEM((half, M, 2 * R), BF16),
            pltpu.VMEM((C, 2, R, H), F32),
            pltpu.VMEM((C, R, H), BF16),
            pltpu.VMEM((C, R, H), BF16),
            pltpu.VMEM((2, far, R, H), BF16),
            pltpu.VMEM((2, far, R, H), BF16),
            pltpu.VMEM((steps, 2 * E, H), F32),
            pltpu.VMEM((steps, 2 * E, H), F32),
            dma((2,)),
            dma((2, far)),
            dma((2, far)),
            dma((2 * far,)),
            dma((2 * far,)),
            dma((half,)),
            dma((half,)),
            dma((C,)),
            dma((C,)),
            dma((2, far)),
            dma((2, far)),
            dma((steps,)),
            dma((steps,)),
        ],
        compiler_params=pltpu.CompilerParams(
            collective_id=0, has_side_effects=True, vmem_limit_bytes=60 * 1024 * 1024
        ),
    )(context, residual, out_weight, in_factor, out_factor, cotangent)


def solution(mesh):
    in_specs = (
        P(None, "fsdp", "member"),
        P("fsdp", "member"),
        P("fsdp", "member"),
        P(None, "member"),
        P(None, "member"),
        P(None, "fsdp", "member"),
    )
    out_specs = (
        P(None, "fsdp", "member"),
        P(None, "fsdp", "member"),
        P("fsdp", "member"),
        P(None, "member"),
        P(None, "member"),
        P("fsdp", "member"),
    )
    members = mesh.shape["member"]
    chips = mesh.shape["fsdp"] // 2
    if members == 2 and chips >= 8 and chips & (chips - 1) == 0:
        per_device = functools.partial(fused, chips)
    else:
        per_device = general
    return jax.shard_map(
        per_device, mesh=mesh, in_specs=in_specs, out_specs=out_specs, check_vma=False
    )
```

```python
import functools

import jax
import jax.numpy as jnp
from jax import lax
from jax.experimental import pallas as pl
from jax.experimental.pallas import tpu as pltpu
from jax.sharding import PartitionSpec as P

F32 = jnp.float32
BF16 = jnp.bfloat16


def general(context, residual, out_weight, in_factor, out_factor, cotangent):
    in_wide = in_factor.astype(jnp.float32)
    out_wide = out_factor.astype(jnp.float32)
    scaled_local = (context.astype(jnp.float32) * in_wide[:, None, :]).astype(jnp.bfloat16)
    scaled_grad = (cotangent.astype(jnp.float32) * out_wide[:, None, :]).astype(jnp.bfloat16)
    scaled_context = lax.all_gather(scaled_local, "member", axis=2, tiled=True)
    weight = lax.all_gather(out_weight, "fsdp", axis=0, tiled=True)
    projected = jnp.einsum(
        "eti,id->etd", scaled_context, weight, preferred_element_type=jnp.float32
    )
    partial_value = jnp.einsum(
        "etd,id->eti", scaled_grad, weight, preferred_element_type=jnp.float32
    )
    hidden = (residual.astype(jnp.float32)[None] + projected * out_wide[:, None, :]).astype(
        jnp.bfloat16
    )
    backward = lax.psum_scatter(
        partial_value.astype(jnp.bfloat16), "member", scatter_dimension=2, tiled=True
    ).astype(jnp.float32)
    grad_context = (backward * in_wide[:, None, :]).astype(jnp.bfloat16)
    grad_in_local = jnp.sum(context.astype(jnp.float32) * backward, axis=1)
    grad_out_local = jnp.sum(cotangent.astype(jnp.float32) * projected, axis=1)
    grad_in, grad_out = lax.psum((grad_in_local, grad_out_local), "fsdp")
    grad_block = jnp.einsum(
        "eti,etd->id", scaled_context, scaled_grad, preferred_element_type=jnp.float32
    )
    grad_weight = lax.psum_scatter(grad_block, "fsdp", scatter_dimension=0, tiled=True)
    grad_residual = jnp.sum(cotangent.astype(jnp.float32), axis=0)
    return (hidden, grad_context, grad_weight, grad_in, grad_out, grad_residual)


def kernel(
    C,
    ctx_h, res, w_h, inf, outf, cot_h,
    hid, gc, gw, gi, go, gr,
    ctx, cot, cbuf, infx, sc, sg, wb, proj, part, xrecv, gall, psend, precv, rsend, rrecv, arb, arr, swp,
    ld_sem, cx_ss, cx_rs, ag_ss, ag_rs, pt_ss, pt_rs, px_ss, px_rs, ps_ss, ps_rs, rs_ss, rs_rs, ar_ss, ar_rs,
):
    E, T, H = ctx.shape
    M = E * T
    R = w_h.shape[0]
    R2 = 2 * R
    S = R // 2
    half = C // 2
    far = C // 2
    bits = []
    b = 1
    while b < 2 * C:
        bits.append(b)
        b *= 2

    m = lax.axis_index("member")
    f = lax.axis_index("fsdp")
    c = f % 2
    q = f // 2
    p = (1 - q % 2) * (q // 2) + (q % 2) * (C - 1 - q // 2)

    def chip_at(offset):
        pos = (p + offset + C) % C
        y = pos // half
        return 2 * ((1 - y) * pos + y * (C - 1 - pos)) + y

    peer = (1 - m, f)
    partner = (m, q * 2 + 1 - c)
    nxt = (m, chip_at(1) * 2 + c)
    prv = (m, chip_at(-1) * 2 + c)
    side = (nxt, prv)
    sign = (1, -1)
    flips = [(m, f + bit * (1 - 2 * ((f // bit) % 2))) for bit in bits]

    def rc(src, dst, ss, rs, dev):
        return pltpu.make_async_remote_copy(
            src_ref=src, dst_ref=dst, send_sem=ss, recv_sem=rs,
            device_id=dev, device_id_type=pl.DeviceIdType.MESH,
        )

    barrier = pltpu.get_barrier_semaphore()
    greet = [peer, nxt, prv] + flips
    for dev in greet:
        pl.semaphore_signal(barrier, inc=1, device_id=dev, device_id_type=pl.DeviceIdType.MESH)

    def rows_of(core):
        return pl.ds(pl.multiple_of(core * R, R), R)

    ld_ctx = pltpu.make_async_copy(ctx_h, ctx, ld_sem.at[0])
    ld_cot = pltpu.make_async_copy(cot_h, cot, ld_sem.at[1])
    ld_w = pltpu.make_async_copy(w_h, wb.at[q, rows_of(c)], ld_sem.at[2])
    ld_ctx.start()
    ld_cot.start()
    ld_w.start()

    inw = inf[...].astype(F32)
    outw = outf[...].astype(F32)

    def cx(e):
        return rc(ctx_h.at[e], cbuf.at[e], cx_ss.at[e], cx_rs.at[e], peer)

    cxf = rc(inf, infx, cx_ss.at[E], cx_rs.at[E], peer)

    def sub(core, u):
        return pl.ds(pl.multiple_of(core * R + u * S, S), S)

    def subs(d, s):
        return (0, 1) if s < far else (d,)

    def ag(d, s, u, shift):
        qq = chip_at(-sign[d] * (s - 1 + shift))
        dst = wb.at[qq, sub(c, u)]
        src = w_h.at[pl.ds(u * S, S)] if (s == 1 and shift == 0) else dst
        return rc(src, dst, ag_ss.at[d, s - 1, u], ag_rs.at[d, s - 1, u], side[d])

    def pt(k, u, offset, mine):
        qq = chip_at(offset)
        dst = wb.at[qq, sub(c if mine else 1 - c, u)]
        src = w_h.at[pl.ds(u * S, S)] if (mine and k == 0) else dst
        return rc(src, dst, pt_ss.at[k, u], pt_rs.at[k, u], partner)

    sends = []

    def go_send(copy):
        copy.start()
        sends.append(copy)

    pl.semaphore_wait(barrier, len(greet))
    go_send(cxf)
    for e in range(E):
        go_send(cx(e))
    for u in range(2):
        for d in range(2):
            go_send(ag(d, 1, u, 0))
        go_send(pt(0, u, 0, True))

    ld_ctx.wait()
    for e in range(E):
        v = (ctx[e].astype(F32) * inw[e:e + 1]).astype(BF16)
        for j in range(half):
            sc[m * half + j, e * T:(e + 1) * T, :] = v[:, j * R2:(j + 1) * R2]
    ld_cot.wait()
    for e in range(E):
        sg[e * T:(e + 1) * T, :] = (cot[e].astype(F32) * outw[e:e + 1]).astype(BF16)
    proj[...] = jnp.zeros(proj.shape, F32)

    def px(qq):
        return rc(part.at[qq], xrecv.at[qq % half], px_ss.at[qq % half], px_rs.at[qq % half], peer)

    def ps(qq):
        return rc(psend.at[qq], precv.at[qq], ps_ss.at[qq], ps_rs.at[qq], partner)

    def gw_half(h):
        def body(j, carry):
            qq = h * half + j
            g = lax.dot_general(sc[qq], sg[...], (((0,), (0,)), ((), ())), preferred_element_type=F32)
            gall[qq, 0] = g[:R]
            gall[qq, 1] = g[R:]
            psend[qq] = gall[qq, 1 - c].astype(BF16)
            ps(qq).start()
            return carry
        lax.fori_loop(0, half, body, 0)

    def project(qq):
        proj[...] += jnp.dot(sc[qq], wb[qq], preferred_element_type=F32)

    def process(offsets):
        def body(j, carry):
            off = offsets[0] if len(offsets) == 1 else offsets[0] + j * (offsets[1] - offsets[0])
            qq = chip_at(off)
            part[qq] = lax.dot_general(
                sg[...], wb[qq], (((1,), (1,)), ((), ())), preferred_element_type=F32
            ).astype(BF16)

            @pl.when(qq // half != m)
            def _():
                px(qq).start()

            @pl.when(qq // half == m)
            def _():
                project(qq)
            return carry
        lax.fori_loop(0, len(offsets), body, 0)

    def rs(d, k, u):
        rows = pl.ds(u * S, S)
        return rc(rsend.at[d, k, rows], rrecv.at[d, k, rows], rs_ss.at[d, k, u], rs_rs.at[d, k, u], side[d])

    def chip_sum(qq, u):
        rows = slice(u * S, (u + 1) * S)
        return gall[qq, c, rows, :] + precv[qq, rows, :].astype(F32)

    def rs_step(k, h):
        if k == 0:
            qf = chip_at(far)

            @pl.when(qf // half == h)
            def _():
                ps(qf).wait_recv()
                for d in range(2):
                    rsend[d, 0, d * S:(d + 1) * S, :] = chip_sum(qf, d).astype(BF16)
                    rs(d, 0, d).start()
            return
        for d in range(2):
            qq = chip_at(sign[d] * (far - k))

            @pl.when(qq // half == h)
            def _():
                ps(qq).wait_recv()
                for u in ((1 - d, d) if k == 1 else (0, 1)):
                    rows = slice(u * S, (u + 1) * S)
                    v = chip_sum(qq, u)
                    if k > 1 or u == d:
                        rs(d, k - 1, u).wait_recv()
                        v = v + rrecv[d, k - 1, rows, :].astype(F32)
                    rsend[d, k, rows, :] = v.astype(BF16)
                    rs(d, k, u).start()

    gw_half(m)
    ld_w.wait()
    for u in range(2):
        pt(0, u, 0, False).wait_recv()
    process([0])
    cxf_in = cxf

    def scale_in(e):
        cx(e).wait_recv()
        v = (cbuf[e].astype(F32) * infx[e:e + 1, :].astype(F32)).astype(BF16)
        for j in range(half):
            sc[(1 - m) * half + j, e * T:(e + 1) * T, :] = v[:, j * R2:(j + 1) * R2]

    for s in range(1, far):
        for u in range(2):
            for d in range(2):
                ag(d, s, u, 1).wait_recv()
                if u in subs(d, s + 1):
                    go_send(ag(d, s + 1, u, 0))
                go_send(pt(d * (far - 1) + s, u, -sign[d] * s, True))
        if s == 1:
            gr[...] = jnp.sum(cot[...].astype(F32), axis=0)
        rs_step(s - 1, m)
        for u in range(2):
            for d in range(2):
                pt(d * (far - 1) + s, u, -sign[d] * s, False).wait_recv()
        process([-s, s])
        if s == 1:
            cxf_in.wait_recv()
        if s >= 2 and s - 2 < E:
            scale_in(s - 2)
    for d in range(2):
        ag(d, far, d, 1).wait_recv()
        go_send(pt(2 * far - 1, d, far, True))
    for d in range(2):
        pt(2 * far - 1, d, far, False).wait_recv()
    process([far])
    for e in range(max(min(far - 2, E), 0), E):
        scale_in(e)
    gw_half(1 - m)
    rs_step(0, 1 - m)
    rs_step(far - 1, m)

    def project_rest(lo, hi):
        def body(j, carry):
            project((1 - m) * half + j)
            return carry
        lax.fori_loop(lo, hi, body, 0)

    project_rest(0, half)
    resw = res[...].astype(F32)
    for e in range(E):
        pe = proj[e * T:(e + 1) * T, :]
        hid[e] = (resw + pe * outw[e:e + 1]).astype(BF16)
        arb[0, 2 * E + e:2 * E + e + 1, :] = jnp.sum(cot[e].astype(F32) * pe, axis=0, keepdims=True)
    rs_step(1, 1 - m)
    for j in range(half):
        cols = slice(j * R2, (j + 1) * R2)
        for e in range(E):
            rows = slice(e * T, (e + 1) * T)
            a = ctx[e, :, cols].astype(F32) * part[m * half + j, rows, :].astype(F32)
            arb[0, e:e + 1, cols] = jnp.sum(a, axis=0, keepdims=True)
            a = cbuf[e, :, cols].astype(F32) * part[(1 - m) * half + j, rows, :].astype(F32)
            arb[0, E + e:E + e + 1, cols] = jnp.sum(a, axis=0, keepdims=True)

    def ar(i):
        return rc(arb.at[i], arr.at[i], ar_ss.at[i], ar_rs.at[i], flips[i])

    swap = rc(swp.at[0], swp.at[1], cx_ss.at[E + 1], cx_rs.at[E + 1], peer)

    def ar_step(i):
        ar(i).wait_recv()
        total = arb[i] + arr[i]
        if i + 1 < len(bits):
            arb[i + 1] = total
            go_send(ar(i + 1))
        else:
            swp[0] = total[E:2 * E]
            go_send(swap)
            gi[...] = total[:E]
            go[...] = total[2 * E:]

    go_send(ar(0))
    ar_step(0)
    done = 1
    for k in range(2, far):
        rs_step(k, 1 - m)
        if done < len(bits):
            ar_step(done)
            done += 1
    while done < len(bits):
        ar_step(done)
        done += 1

    ps(q).wait_recv()
    for u in range(2):
        rows = slice(u * S, (u + 1) * S)
        own = chip_sum(q, u)
        for d in range(2):
            rs(d, far - 1, u).wait_recv()
            own = own + rrecv[d, far - 1, rows, :].astype(F32)
        gw[rows, :] = own

    for j in range(half):
        rc(xrecv.at[j], xrecv.at[j], px_ss.at[j], px_rs.at[j], peer).wait_recv()
        cols = slice(j * R2, (j + 1) * R2)
        for e in range(E):
            rows = slice(e * T, (e + 1) * T)
            be = part[m * half + j, rows, :].astype(F32) + xrecv[j, rows, :].astype(F32)
            gc[e, :, cols] = (be * inw[e:e + 1, cols]).astype(BF16)

    swap.wait_recv()
    gi[...] += swp[1]

    for copy in sends:
        copy.wait_send()
    for d in range(2):
        for k in range(far):
            for u in ((d,) if k == 0 else (0, 1)):
                rs(d, k, u).wait_send()

    def drain(j, carry):
        ps(j).wait_send()
        return carry
    lax.fori_loop(0, C, drain, 0)
    for j in range(half):
        rc(part.at[(1 - m) * half + j], xrecv.at[j], px_ss.at[j], px_rs.at[j], peer).wait_send()


def fused(C, context, residual, out_weight, in_factor, out_factor, cotangent):
    E, T, H = context.shape
    M = E * T
    R = out_weight.shape[0]
    half = C // 2
    far = half
    steps = (2 * C).bit_length() - 1
    vm = pl.BlockSpec(memory_space=pltpu.VMEM)
    hbm = pl.BlockSpec(memory_space=pl.ANY)
    dma = pltpu.SemaphoreType.DMA
    shape = jax.ShapeDtypeStruct
    return pl.pallas_call(
        functools.partial(kernel, C),
        out_shape=(
            shape((E, T, H), BF16),
            shape((E, T, H), BF16),
            shape((R, H), F32),
            shape((E, H), F32),
            shape((E, H), F32),
            shape((T, H), F32),
        ),
        in_specs=[hbm, vm, hbm, vm, vm, hbm],
        out_specs=tuple([vm] * 6),
        scratch_shapes=[
            pltpu.VMEM((E, T, H), BF16),
            pltpu.VMEM((E, T, H), BF16),
            pltpu.VMEM((E, T, H), BF16),
            pltpu.VMEM((E, H), BF16),
            pltpu.VMEM((C, M, 2 * R), BF16),
            pltpu.VMEM((M, H), BF16),
            pltpu.VMEM((C, 2 * R, H), BF16),
            pltpu.VMEM((M, H), F32),
            pltpu.VMEM((C, M, 2 * R), BF16),
            pltpu.VMEM((half, M, 2 * R), BF16),
            pltpu.VMEM((C, 2, R, H), F32),
            pltpu.VMEM((C, R, H), BF16),
            pltpu.VMEM((C, R, H), BF16),
            pltpu.VMEM((2, far, R, H), BF16),
            pltpu.VMEM((2, far, R, H), BF16),
            pltpu.VMEM((steps, 3 * E, H), F32),
            pltpu.VMEM((steps, 3 * E, H), F32),
            pltpu.VMEM((2, E, H), F32),
            dma((3,)),
            dma((E + 2,)),
            dma((E + 2,)),
            dma((2, far, 2)),
            dma((2, far, 2)),
            dma((2 * far, 2)),
            dma((2 * far, 2)),
            dma((half,)),
            dma((half,)),
            dma((C,)),
            dma((C,)),
            dma((2, far, 2)),
            dma((2, far, 2)),
            dma((steps,)),
            dma((steps,)),
        ],
        compiler_params=pltpu.CompilerParams(
            collective_id=0, has_side_effects=True, vmem_limit_bytes=60 * 1024 * 1024
        ),
    )(context, residual, out_weight, in_factor, out_factor, cotangent)


def solution(mesh):
    in_specs = (
        P(None, "fsdp", "member"),
        P("fsdp", "member"),
        P("fsdp", "member"),
        P(None, "member"),
        P(None, "member"),
        P(None, "fsdp", "member"),
    )
    out_specs = (
        P(None, "fsdp", "member"),
        P(None, "fsdp", "member"),
        P("fsdp", "member"),
        P(None, "member"),
        P(None, "member"),
        P("fsdp", "member"),
    )
    members = mesh.shape["member"]
    chips = mesh.shape["fsdp"] // 2
    if members == 2 and chips >= 8 and chips & (chips - 1) == 0:
        per_device = functools.partial(fused, chips)
    else:
        per_device = general
    return jax.shard_map(
        per_device, mesh=mesh, in_specs=in_specs, out_specs=out_specs, check_vma=False
    )
```

```python
import functools

import jax
import jax.numpy as jnp
from jax import lax
from jax.experimental import pallas as pl
from jax.experimental.pallas import tpu as pltpu
from jax.sharding import PartitionSpec as P

F32 = jnp.float32
BF16 = jnp.bfloat16


def general(context, residual, out_weight, in_factor, out_factor, cotangent):
    in_wide = in_factor.astype(jnp.float32)
    out_wide = out_factor.astype(jnp.float32)
    scaled_local = (context.astype(jnp.float32) * in_wide[:, None, :]).astype(jnp.bfloat16)
    scaled_grad = (cotangent.astype(jnp.float32) * out_wide[:, None, :]).astype(jnp.bfloat16)
    scaled_context = lax.all_gather(scaled_local, "member", axis=2, tiled=True)
    weight = lax.all_gather(out_weight, "fsdp", axis=0, tiled=True)
    projected = jnp.einsum(
        "eti,id->etd", scaled_context, weight, preferred_element_type=jnp.float32
    )
    partial_value = jnp.einsum(
        "etd,id->eti", scaled_grad, weight, preferred_element_type=jnp.float32
    )
    hidden = (residual.astype(jnp.float32)[None] + projected * out_wide[:, None, :]).astype(
        jnp.bfloat16
    )
    backward = lax.psum_scatter(
        partial_value.astype(jnp.bfloat16), "member", scatter_dimension=2, tiled=True
    ).astype(jnp.float32)
    grad_context = (backward * in_wide[:, None, :]).astype(jnp.bfloat16)
    grad_in_local = jnp.sum(context.astype(jnp.float32) * backward, axis=1)
    grad_out_local = jnp.sum(cotangent.astype(jnp.float32) * projected, axis=1)
    grad_in, grad_out = lax.psum((grad_in_local, grad_out_local), "fsdp")
    grad_block = jnp.einsum(
        "eti,etd->id", scaled_context, scaled_grad, preferred_element_type=jnp.float32
    )
    grad_weight = lax.psum_scatter(grad_block, "fsdp", scatter_dimension=0, tiled=True)
    grad_residual = jnp.sum(cotangent.astype(jnp.float32), axis=0)
    return (hidden, grad_context, grad_weight, grad_in, grad_out, grad_residual)


def kernel(
    C,
    ctx_h, res, w_h, inf, outf, cot_h,
    hid, gc, gw, gi, go, gr,
    ctx, cot, cbuf, infx, sc, sg, wb, proj, part, xrecv, gall, psend, precv, rsend, rrecv, arb, arr, swp,
    ld_sem, cx_ss, cx_rs, ag_ss, ag_rs, pt_ss, pt_rs, px_ss, px_rs, ps_ss, ps_rs, rs_ss, rs_rs, ar_ss, ar_rs,
):
    E, T, H = ctx.shape
    M = E * T
    R = w_h.shape[0]
    R2 = 2 * R
    S = R // 2
    half = C // 2
    far = C // 2
    bits = []
    b = 1
    while b < 2 * C:
        bits.append(b)
        b *= 2

    m = lax.axis_index("member")
    f = lax.axis_index("fsdp")
    c = f % 2
    q = f // 2
    p = (1 - q % 2) * (q // 2) + (q % 2) * (C - 1 - q // 2)

    def chip_at(offset):
        pos = (p + offset + C) % C
        y = pos // half
        return 2 * ((1 - y) * pos + y * (C - 1 - pos)) + y

    peer = (1 - m, f)
    partner = (m, q * 2 + 1 - c)
    nxt = (m, chip_at(1) * 2 + c)
    prv = (m, chip_at(-1) * 2 + c)
    side = (nxt, prv)
    sign = (1, -1)
    flips = [(m, f + bit * (1 - 2 * ((f // bit) % 2))) for bit in bits]

    def rc(src, dst, ss, rs, dev):
        return pltpu.make_async_remote_copy(
            src_ref=src, dst_ref=dst, send_sem=ss, recv_sem=rs,
            device_id=dev, device_id_type=pl.DeviceIdType.MESH,
        )

    barrier = pltpu.get_barrier_semaphore()
    greet = [peer, nxt, prv] + flips
    for dev in greet:
        pl.semaphore_signal(barrier, inc=1, device_id=dev, device_id_type=pl.DeviceIdType.MESH)

    def rows_of(core):
        return pl.ds(pl.multiple_of(core * R, R), R)

    ld_ctx = pltpu.make_async_copy(ctx_h, ctx, ld_sem.at[0])
    ld_cot = pltpu.make_async_copy(cot_h, cot, ld_sem.at[1])
    ld_w = pltpu.make_async_copy(w_h, wb.at[q, rows_of(c)], ld_sem.at[2])
    ld_ctx.start()
    ld_cot.start()
    ld_w.start()

    inw = inf[...].astype(F32)
    outw = outf[...].astype(F32)

    def cx(e):
        return rc(ctx_h.at[:, :, pl.ds(e * R2, R2)], cbuf.at[e], cx_ss.at[e], cx_rs.at[e], peer)

    cxf = rc(inf, infx, cx_ss.at[half], cx_rs.at[half], peer)

    def sub(core, u):
        return pl.ds(pl.multiple_of(core * R + u * S, S), S)

    def subs(d, s):
        return (0, 1) if s < far else (d,)

    def ag(d, s, u, shift):
        qq = chip_at(-sign[d] * (s - 1 + shift))
        dst = wb.at[qq, sub(c, u)]
        src = w_h.at[pl.ds(u * S, S)] if (s == 1 and shift == 0) else dst
        return rc(src, dst, ag_ss.at[d, s - 1, u], ag_rs.at[d, s - 1, u], side[d])

    def pt(k, u, offset, mine):
        qq = chip_at(offset)
        dst = wb.at[qq, sub(c if mine else 1 - c, u)]
        src = w_h.at[pl.ds(u * S, S)] if (mine and k == 0) else dst
        return rc(src, dst, pt_ss.at[k, u], pt_rs.at[k, u], partner)

    sends = []

    def go_send(copy):
        copy.start()
        sends.append(copy)

    pl.semaphore_wait(barrier, len(greet))
    go_send(cxf)
    for j in range(half):
        go_send(cx(j))
    for u in range(2):
        for d in range(2):
            go_send(ag(d, 1, u, 0))
        go_send(pt(0, u, 0, True))

    ld_ctx.wait()
    for e in range(E):
        v = (ctx[e].astype(F32) * inw[e:e + 1]).astype(BF16)
        for j in range(half):
            sc[m * half + j, e * T:(e + 1) * T, :] = v[:, j * R2:(j + 1) * R2]
    ld_cot.wait()
    for e in range(E):
        sg[e * T:(e + 1) * T, :] = (cot[e].astype(F32) * outw[e:e + 1]).astype(BF16)
    proj[...] = jnp.zeros(proj.shape, F32)

    def px(qq):
        return rc(part.at[qq], xrecv.at[qq % half], px_ss.at[qq % half], px_rs.at[qq % half], peer)

    def ps(qq):
        return rc(psend.at[qq], precv.at[qq], ps_ss.at[qq], ps_rs.at[qq], partner)

    def gw_one(qq):
        g = lax.dot_general(sc[qq], sg[...], (((0,), (0,)), ((), ())), preferred_element_type=F32)
        gall[qq, 0] = g[:R]
        gall[qq, 1] = g[R:]
        psend[qq] = gall[qq, 1 - c].astype(BF16)
        ps(qq).start()

    def gw_half(h):
        def body(j, carry):
            gw_one(h * half + j)
            return carry
        lax.fori_loop(0, half, body, 0)

    def project(qq):
        proj[...] += jnp.dot(sc[qq], wb[qq], preferred_element_type=F32)

    def process(offsets):
        def body(j, carry):
            off = offsets[0] if len(offsets) == 1 else offsets[0] + j * (offsets[1] - offsets[0])
            qq = chip_at(off)
            part[qq] = lax.dot_general(
                sg[...], wb[qq], (((1,), (1,)), ((), ())), preferred_element_type=F32
            ).astype(BF16)

            @pl.when(qq // half != m)
            def _():
                px(qq).start()

            @pl.when(qq // half == m)
            def _():
                project(qq)
            return carry
        lax.fori_loop(0, len(offsets), body, 0)

    def rs(d, k, u):
        rows = pl.ds(u * S, S)
        return rc(rsend.at[d, k, rows], rrecv.at[d, k, rows], rs_ss.at[d, k, u], rs_rs.at[d, k, u], side[d])

    def chip_sum(qq, u):
        rows = slice(u * S, (u + 1) * S)
        return gall[qq, c, rows, :] + precv[qq, rows, :].astype(F32)

    def rs_step(k):
        if k == 0:
            qf = chip_at(far)
            ps(qf).wait_recv()
            for d in range(2):
                rsend[d, 0, d * S:(d + 1) * S, :] = chip_sum(qf, d).astype(BF16)
                go_send(rs(d, 0, d))
            return
        qs = [chip_at(sign[d] * (far - k)) for d in range(2)]
        for d in range(2):
            ps(qs[d]).wait_recv()
        for i in range(2):
            for d in range(2):
                u = (1 - d if i == 0 else d) if k == 1 else i
                rows = slice(u * S, (u + 1) * S)
                v = chip_sum(qs[d], u)
                if k > 1 or u == d:
                    rs(d, k - 1, u).wait_recv()
                    v = v + rrecv[d, k - 1, rows, :].astype(F32)
                rsend[d, k, rows, :] = v.astype(BF16)
                go_send(rs(d, k, u))

    gw_half(m)
    ld_w.wait()
    for u in range(2):
        pt(0, u, 0, False).wait_recv()
    process([0])
    cxf_in = cxf

    def scale_in(j):
        cx(j).wait_recv()
        for e in range(E):
            wide = infx[e:e + 1, j * R2:(j + 1) * R2].astype(F32)
            sc[(1 - m) * half + j, e * T:(e + 1) * T, :] = (cbuf[j, e].astype(F32) * wide).astype(BF16)
        gw_one((1 - m) * half + j)

    for s in range(1, far):
        for u in range(2):
            for d in range(2):
                ag(d, s, u, 1).wait_recv()
                if u in subs(d, s + 1):
                    go_send(ag(d, s + 1, u, 0))
                go_send(pt(d * (far - 1) + s, u, -sign[d] * s, True))
        if s == 1:
            gr[...] = jnp.sum(cot[...].astype(F32), axis=0)
        for u in range(2):
            for d in range(2):
                pt(d * (far - 1) + s, u, -sign[d] * s, False).wait_recv()
        process([-s, s])
        if s == 1:
            cxf_in.wait_recv()
        if s >= 2:
            scale_in(s - 2)
    for d in range(2):
        ag(d, far, d, 1).wait_recv()
        go_send(pt(2 * far - 1, d, far, True))
    for d in range(2):
        pt(2 * far - 1, d, far, False).wait_recv()
    process([far])
    for j in range(far - 2, half):
        scale_in(j)
    rs_step(0)

    def project_rest(lo, hi):
        def body(j, carry):
            project((1 - m) * half + j)
            return carry
        lax.fori_loop(lo, hi, body, 0)

    project_rest(0, half)
    rs_step(1)
    resw = res[...].astype(F32)
    for e in range(E):
        pe = proj[e * T:(e + 1) * T, :]
        hid[e] = (resw + pe * outw[e:e + 1]).astype(BF16)
        arb[0, 2 * E + e:2 * E + e + 1, :] = jnp.sum(cot[e].astype(F32) * pe, axis=0, keepdims=True)
    for j in range(half):
        cols = slice(j * R2, (j + 1) * R2)
        for e in range(E):
            rows = slice(e * T, (e + 1) * T)
            a = ctx[e, :, cols].astype(F32) * part[m * half + j, rows, :].astype(F32)
            arb[0, e:e + 1, cols] = jnp.sum(a, axis=0, keepdims=True)
            a = cbuf[j, e].astype(F32) * part[(1 - m) * half + j, rows, :].astype(F32)
            arb[0, E + e:E + e + 1, cols] = jnp.sum(a, axis=0, keepdims=True)

    def ar(i):
        return rc(arb.at[i], arr.at[i], ar_ss.at[i], ar_rs.at[i], flips[i])

    swap = rc(swp.at[0], swp.at[1], cx_ss.at[half + 1], cx_rs.at[half + 1], peer)

    def ar_step(i):
        ar(i).wait_recv()
        total = arb[i] + arr[i]
        if i + 1 < len(bits):
            arb[i + 1] = total
            go_send(ar(i + 1))
        else:
            swp[0] = total[E:2 * E]
            go_send(swap)
            gi[...] = total[:E]
            go[...] = total[2 * E:]

    go_send(ar(0))
    ar_step(0)
    done = 1
    for k in range(2, far):
        rs_step(k)
        if done < len(bits):
            ar_step(done)
            done += 1
    while done < len(bits):
        ar_step(done)
        done += 1

    ps(q).wait_recv()
    for u in range(2):
        rows = slice(u * S, (u + 1) * S)
        own = chip_sum(q, u)
        for d in range(2):
            rs(d, far - 1, u).wait_recv()
            own = own + rrecv[d, far - 1, rows, :].astype(F32)
        gw[rows, :] = own

    for j in range(half):
        rc(xrecv.at[j], xrecv.at[j], px_ss.at[j], px_rs.at[j], peer).wait_recv()
        cols = slice(j * R2, (j + 1) * R2)
        for e in range(E):
            rows = slice(e * T, (e + 1) * T)
            be = part[m * half + j, rows, :].astype(F32) + xrecv[j, rows, :].astype(F32)
            gc[e, :, cols] = (be * inw[e:e + 1, cols]).astype(BF16)

    swap.wait_recv()
    gi[...] += swp[1]

    for copy in sends:
        copy.wait_send()

    def drain(j, carry):
        ps(j).wait_send()
        return carry
    lax.fori_loop(0, C, drain, 0)
    for j in range(half):
        rc(part.at[(1 - m) * half + j], xrecv.at[j], px_ss.at[j], px_rs.at[j], peer).wait_send()


def fused(C, context, residual, out_weight, in_factor, out_factor, cotangent):
    E, T, H = context.shape
    M = E * T
    R = out_weight.shape[0]
    half = C // 2
    far = half
    steps = (2 * C).bit_length() - 1
    vm = pl.BlockSpec(memory_space=pltpu.VMEM)
    hbm = pl.BlockSpec(memory_space=pl.ANY)
    dma = pltpu.SemaphoreType.DMA
    shape = jax.ShapeDtypeStruct
    results = pl.pallas_call(
        functools.partial(kernel, C),
        out_shape=(
            shape((E, T, H), BF16),
            shape((E, T, H), BF16),
            shape((R, H), F32),
            shape((E, H), F32),
            shape((E, H), F32),
            shape((T, H), F32),
        ),
        in_specs=[hbm, vm, hbm, vm, vm, hbm],
        out_specs=tuple([vm] * 6),
        scratch_shapes=[
            pltpu.VMEM((E, T, H), BF16),
            pltpu.VMEM((E, T, H), BF16),
            pltpu.VMEM((half, E, T, 2 * R), BF16),
            pltpu.VMEM((E, H), BF16),
            pltpu.VMEM((C, M, 2 * R), BF16),
            pltpu.VMEM((M, H), BF16),
            pltpu.VMEM((C, 2 * R, H), BF16),
            pltpu.VMEM((M, H), F32),
            pltpu.VMEM((C, M, 2 * R), BF16),
            pltpu.VMEM((half, M, 2 * R), BF16),
            pltpu.VMEM((C, 2, R, H), F32),
            pltpu.VMEM((C, R, H), BF16),
            pltpu.VMEM((C, R, H), BF16),
            pltpu.VMEM((2, far, R, H), BF16),
            pltpu.VMEM((2, far, R, H), BF16),
            pltpu.VMEM((steps, 3 * E, H), F32),
            pltpu.VMEM((steps, 3 * E, H), F32),
            pltpu.VMEM((2, E, H), F32),
            dma((3,)),
            dma((half + 2,)),
            dma((half + 2,)),
            dma((2, far, 2)),
            dma((2, far, 2)),
            dma((2 * far, 2)),
            dma((2 * far, 2)),
            dma((half,)),
            dma((half,)),
            dma((C,)),
            dma((C,)),
            dma((2, far, 2)),
            dma((2, far, 2)),
            dma((steps,)),
            dma((steps,)),
        ],
        compiler_params=pltpu.CompilerParams(
            collective_id=0, has_side_effects=True, vmem_limit_bytes=60 * 1024 * 1024
        ),
    )(context, residual, out_weight, in_factor, out_factor, cotangent)
    return pl.pallas_call(
        deliver,
        out_shape=tuple(shape(r.shape, r.dtype) for r in results),
        in_specs=[hbm] * 6,
        out_specs=tuple([hbm] * 6),
        scratch_shapes=[pltpu.VMEM(r.shape, r.dtype) for r in results] + [dma((2, 6))],
    )(*results)


def deliver(*refs):
    sources, results, held, sem = refs[:6], refs[6:12], refs[12:18], refs[18]
    loads = [pltpu.make_async_copy(sources[i], held[i], sem.at[0, i]) for i in range(6)]
    stores = [pltpu.make_async_copy(held[i], results[i], sem.at[1, i]) for i in range(6)]
    for copy in loads:
        copy.start()
    for i in range(6):
        loads[i].wait()
        stores[i].start()
    for copy in stores:
        copy.wait()


def solution(mesh):
    in_specs = (
        P(None, "fsdp", "member"),
        P("fsdp", "member"),
        P("fsdp", "member"),
        P(None, "member"),
        P(None, "member"),
        P(None, "fsdp", "member"),
    )
    out_specs = (
        P(None, "fsdp", "member"),
        P(None, "fsdp", "member"),
        P("fsdp", "member"),
        P(None, "member"),
        P(None, "member"),
        P("fsdp", "member"),
    )
    members = mesh.shape["member"]
    chips = mesh.shape["fsdp"] // 2
    if members == 2 and chips >= 8 and chips & (chips - 1) == 0:
        per_device = functools.partial(fused, chips)
    else:
        per_device = general
    return jax.shard_map(
        per_device, mesh=mesh, in_specs=in_specs, out_specs=out_specs, check_vma=False
    )
```
